256 devices in a mesh: fibre: 2 (over core), chan: 128 (over z, x, y).
Axes of the slice: x: 4, y: 4, z: 8, core: 2. Of those that a mesh axis runs over, the one named last changes fastest.
Arguments:
- raw: bfloat16 [32768, 4096], P(('fibre', 'chan'))
- starts: int32 [4], replicated, may hold values from 0 to 3072, as said below
- ref_ids: int32 [64], replicated, may hold values from 0 to 32767, as said below
- near_ids: int32 [32768, 8], P(('fibre', 'chan')), may hold values from 0 to 32767, as said below
- cross_ids: int32 [32768, 2], P(('fibre', 'chan')), may hold values from 0 to 255
- cross_mask: int32 [32768, 2], P(('fibre', 'chan')), may hold values 0 or 1
- export_loc: int32 [256], P(('fibre', 'chan')), may hold values from 0 to 127
Outputs:
- correlations: bfloat16 [32768, 64, 512], P(('fibre', 'chan'))
The draws below stay inside these ranges and needn't reach their ends.
Inputs may be any that keep to these rules, and one draw needn't show every extreme that they name: starts[3] is 3072. `ref_ids`: distinct channel ids. `near_ids`: each neighbour lies on the same route as its channel (route = id // 16384) and at most 16 channels away from it.
All inputs are finite; a program needn't handle non-finite values. No bound on the sum of `cross_mask` on one device may be relied on, other than what follows from the above.
Results may differ from the reference program's by a relative error of at most 0.0063.
The reference program's roundings to bfloat16 on the way count: a program that leaves them out, or rounds other values in their place, can miss the bound.
Values may be sent and summed in bfloat16 or wider, within the bound.
A program may use at most 128 MiB of HBM per device.

```python
import math
import jax
import jax.numpy as jnp
from jax import lax

CH_DEV = 128
SAMPLES = 4096
SEG = 1024
SEGS = 4
REFS = 64
LAGS = 512
NN = 8
HALO = 16
XN = 2
XLOC = 1
CHANNELS = 32768
POOL = 256


def draw_raw(key, part):
    key_noise, key_scale = jax.random.split(key, 2)
    noise = jax.random.normal(key_noise, (CHANNELS, SAMPLES), jnp.float32)
    colored = noise + 0.8 * jnp.roll(noise, 1, axis=1) - 0.5 * jnp.roll(noise, 2, axis=1)
    scale = jnp.exp(jax.random.uniform(key_scale, (CHANNELS, 1), jnp.float32, 0.0, math.log(10.0)))
    return (colored * scale).astype(jnp.bfloat16)


def draw_starts(key, part):
    inner = jax.random.randint(jax.random.fold_in(key, 3), (SEGS,), 0, SAMPLES - SEG + 1)
    inner = inner.at[SEGS - 1].set(SAMPLES - SEG)
    return inner.astype(jnp.int32)


def draw_ref_ids(key, part):
    spacing = CHANNELS // REFS
    jitter = jax.random.randint(key, (REFS,), 0, spacing)
    return (jnp.arange(REFS, dtype=jnp.int32) * spacing + jitter).astype(jnp.int32)


def draw_near_ids(key, part):
    key_off = jax.random.fold_in(jax.random.fold_in(key, 7), 0)
    offset = jax.random.randint(key_off, (CHANNELS, NN), -HALO, HALO + 1)
    offset = offset.at[:, 0].set(HALO)
    chan = jnp.arange(CHANNELS, dtype=jnp.int32)[:, None]
    route_len = CHANNELS // 2
    position = chan % route_len
    target = position + offset
    outside = (target < 0) | (target >= route_len)
    target = jnp.where(outside, position - offset, target)
    return (chan - position + target).astype(jnp.int32)


def touch_ends(values, key, least, high):
    longest = values.shape.index(max(values.shape))
    spots = []
    for shift in (0, 1):
        where = [jax.random.randint(jax.random.fold_in(key, axis), (), 0, length) for axis, length in enumerate(values.shape)]
        where[longest] = (where[longest] + shift) % values.shape[longest]
        spots.append(tuple(where))
    return values.at[spots[0]].set(least).at[spots[1]].set(high)


def setup_inputs(seed: int = 0) -> dict:
    key_of = jax.random.split(jax.random.key(seed), 8)
    raw = draw_raw(jax.random.fold_in(key_of[7], 71), 0)
    starts = draw_starts(jax.random.fold_in(key_of[7], 71), 0)
    ref_ids = draw_ref_ids(jax.random.fold_in(key_of[7], 71), 0)
    near_ids = draw_near_ids(jax.random.fold_in(key_of[7], 71), 0)
    cross_ids = touch_ends(jax.random.randint(key_of[4], (CHANNELS, XN), 0, POOL), jax.random.fold_in(key_of[4], 1), 0, POOL - 1).astype(jnp.int32)
    cross_mask = touch_ends((jax.random.randint(key_of[5], (CHANNELS, XN), 0, 2) < 1).astype(jnp.int32), jax.random.fold_in(key_of[5], 1), 0, 1)
    export_loc = touch_ends(jax.random.randint(key_of[6], (POOL,), 0, CH_DEV), jax.random.fold_in(key_of[6], 1), 0, CH_DEV - 1).astype(jnp.int32)
    return {"raw": raw, "starts": starts, "ref_ids": ref_ids, "near_ids": near_ids, "cross_ids": cross_ids, "cross_mask": cross_mask, "export_loc": export_loc}


def make_kernel():
    nbins = SEG // 2
    freq = jnp.arange(nbins, dtype=jnp.int32)
    lag = jnp.arange(LAGS, dtype=jnp.int32) - LAGS // 2
    phase = jnp.mod(freq[:, None] * lag[None, :], SEG).astype(jnp.float32)
    theta = phase * (2.0 * math.pi / SEG)
    scale = 1.0 / math.sqrt(nbins)
    table = jnp.concatenate([jnp.cos(theta) * scale, -jnp.sin(theta) * scale], 0)
    return table.astype(jnp.bfloat16)

def forward_table():
    nbins = SEG // 2
    sample = jnp.arange(SEG, dtype=jnp.int32)
    freq = jnp.arange(nbins, dtype=jnp.int32)
    phase = jnp.mod(sample[:, None] * freq[None, :], SEG).astype(jnp.float32)
    theta = phase * (2.0 * math.pi / SEG)
    keep = (freq > 0).astype(jnp.float32)[None, :]
    return jnp.concatenate([jnp.cos(theta) * keep, -jnp.sin(theta)], 1).astype(jnp.bfloat16)

def spectra_block(rows, starts, table_f):
    nbins = SEG // 2
    pieces = [lax.dynamic_slice_in_dim(rows, starts[s], SEG, 1) for s in range(SEGS)]
    segment = jnp.stack(pieces, 1).astype(jnp.float32)
    count = segment.shape[0] * SEGS
    flat = jnp.dot(segment.reshape(count, SEG), table_f, preferred_element_type=jnp.float32)
    flat = flat.reshape(segment.shape[0], SEGS, SEG)
    power = lax.optimization_barrier(jnp.sum(flat * flat, -1, keepdims=True)) / nbins
    return (flat / jnp.sqrt(power + 1e-06)).astype(jnp.bfloat16)

def reference(raw, starts, ref_ids, near_ids, cross_ids, cross_mask, export_loc):
    nbins = SEG // 2
    total_ch = raw.shape[0]
    table_f = forward_table().astype(jnp.float32)
    first_block = math.gcd(total_ch, 1024)
    spec = lax.map(lambda rows: spectra_block(rows, starts, table_f), raw.reshape(total_ch // first_block, first_block, SAMPLES))
    spec = spec.reshape(total_ch, SEGS, SEG)
    references = spec[ref_ids]
    pool_ids = jnp.arange(POOL, dtype=jnp.int32) // XLOC * CH_DEV + export_loc
    pool = spec[pool_ids]
    kernel = make_kernel()
    ref_f = references.astype(jnp.float32)
    ref_re = ref_f[..., :nbins]
    ref_im = ref_f[..., nbins:]

    def one_block(items):
        own, near_blk, cross_blk, mask_blk = items
        total = own.astype(jnp.float32) + lax.optimization_barrier(jnp.sum(spec[near_blk].astype(jnp.float32), 1))
        mask_f = mask_blk.astype(jnp.float32)
        total = total + lax.optimization_barrier(jnp.sum(pool[cross_blk].astype(jnp.float32) * mask_f[:, :, None, None], 1))
        count = 1.0 + NN + lax.optimization_barrier(jnp.sum(mask_f, 1))
        smoothed = (total / count[:, None, None]).astype(jnp.bfloat16).astype(jnp.float32)
        a_re = smoothed[..., :nbins]
        a_im = smoothed[..., nbins:]
        g_re = jnp.einsum('csf,rsf->crf', a_re, ref_re) + jnp.einsum('csf,rsf->crf', a_im, ref_im)
        g_im = jnp.einsum('csf,rsf->crf', a_im, ref_re) - jnp.einsum('csf,rsf->crf', a_re, ref_im)
        cross = (jnp.concatenate([g_re, g_im], -1) / SEGS).astype(jnp.bfloat16)
        rows = cross.shape[0] * cross.shape[1]
        out = jnp.dot(cross.reshape(rows, SEG), kernel, preferred_element_type=jnp.float32)
        return out.astype(jnp.bfloat16).reshape(cross.shape[0], REFS, LAGS)
    block = math.gcd(total_ch, 256)
    count_b = total_ch // block
    result = lax.map(one_block, (spec.reshape(count_b, block, SEGS, SEG), near_ids.reshape(count_b, block, NN), cross_ids.reshape(count_b, block, XN), cross_mask.reshape(count_b, block, XN)))
    return result.reshape(total_ch, REFS, LAGS)
```

```python
import functools

import jax
import jax.numpy as jnp
import numpy as np
from jax import lax
from jax.experimental import pallas as pl
from jax.experimental.pallas import tpu as pltpu
from jax.sharding import PartitionSpec as P

SEG = 1024
SEGS = 4
REFS = 64
LAGS = 512
NN = 8
XN = 2
HALO = 16
CH = 128
NZ, NA, NB = 8, 4, 4
ROWS = SEGS * SEG // 128
GROUP = 16
MESH = pl.DeviceIdType.MESH
BF = jnp.bfloat16
F32 = jnp.float32


def forward_table():
    phase = (np.arange(SEG)[:, None] * np.arange(SEG // 2)[None, :]) % SEG
    theta = phase * (2.0 * np.pi / SEG)
    keep = (np.arange(SEG // 2) > 0)[None, :]
    return np.concatenate([np.cos(theta) * keep, -np.sin(theta)], 1).astype(BF)


def lag_table():
    phase = (np.arange(SEG // 2)[:, None] * (np.arange(LAGS) - LAGS // 2)[None, :]) % SEG
    theta = phase * (2.0 * np.pi / SEG)
    scale = 1.0 / np.sqrt(SEG // 2)
    table = np.concatenate([np.cos(theta) * scale, -np.sin(theta) * scale], 0).astype(BF)
    return (table.astype(np.float32) / SEGS).astype(BF)


def spectra_kernel(starts, ref_ids, export_loc, raw, table, white, export, picked, padded, seg, wide):
    base = (lax.axis_index("fibre") * (NZ * NA * NB) + lax.axis_index("chan")) * CH
    padded[:, : SEGS * SEG] = raw[...].astype(F32)
    padded[:, SEGS * SEG :] = jnp.zeros((CH, 128), F32)
    for s in range(SEGS):
        start = starts[s]
        first = pl.multiple_of((start // 128) * 128, 128)
        window = padded[:, pl.ds(first, SEG + 128)]
        turn = (SEG + 128) - (start - first)
        turned = pltpu.roll(window, turn, 1)
        seg[s * CH : (s + 1) * CH, :] = turned[:, :SEG].astype(BF)
    for s in range(SEGS):
        spectrum = jnp.dot(
            seg[s * CH : (s + 1) * CH, :], table[...], preferred_element_type=F32
        )
        power = jnp.sum(spectrum * spectrum, -1, keepdims=True) / (SEG // 2)
        spectrum = spectrum / jnp.sqrt(power + 1e-06)
        for j in range(SEG // 128):
            wide[pl.ds(s * 8 + j, CH, stride=ROWS), :] = spectrum[:, j * 128 : (j + 1) * 128]
    white[...] = wide[...].reshape(CH, ROWS, 128).astype(BF)
    export[0] = white[export_loc[0]]
    for r in range(REFS):
        local = ref_ids[r] - base
        mine = ((local >= 0) & (local < CH)).astype(F32)
        row = white[jnp.clip(local, 0, CH - 1)]
        picked[r] = (row.astype(F32) * mine).astype(BF)


def spectra(starts, ref_ids, export_loc, raw):
    smem = pl.BlockSpec(memory_space=pltpu.SMEM)
    vmem = pl.BlockSpec(memory_space=pltpu.VMEM)
    return pl.pallas_call(
        spectra_kernel,
        name="spectra",
        in_specs=[smem, smem, smem, vmem, vmem],
        out_specs=[vmem, vmem, vmem],
        out_shape=[
            jax.ShapeDtypeStruct((CH, ROWS, 128), BF),
            jax.ShapeDtypeStruct((1, ROWS, 128), BF),
            jax.ShapeDtypeStruct((REFS, ROWS, 128), BF),
        ],
        scratch_shapes=[
            pltpu.VMEM((CH, SEGS * SEG + 128), F32),
            pltpu.VMEM((CH * SEGS, SEG), BF),
            pltpu.VMEM((CH * ROWS, 128), F32),
        ],
        compiler_params=pltpu.CompilerParams(vmem_limit_bytes=40 << 20),
    )(starts, ref_ids, export_loc, raw, jnp.asarray(forward_table()))


def exchange_kernel(
    white, export, picked, halo, pool, refs,
    core_in, half, a_in, a_sum, b_in, b_sum, z_in, send, recv, core_send, core_recv,
):
    k = lax.axis_index("fibre")
    chan = lax.axis_index("chan")
    z, x, y = chan // (NA * NB), (chan // NB) % NA, chan % NB
    a = x * (1 - k) + y * k
    b = y * (1 - k) + x * k

    def at(zz, aa, bb):
        return zz * (NA * NB) + (aa * NB + bb) * (1 - k) + (bb * NB + aa) * k

    z_peer = [at((z + j) % NZ, a, b) for j in range(1, NZ)]
    a_peer = [at(z, (a + j) % NA, b) for j in range(1, NA)]
    b_peer = [at(z, a, (b + j) % NB) for j in range(1, NB)]
    up = (chan + 1) % (NZ * NA * NB)
    down = (chan + (NZ * NA * NB) - 1) % (NZ * NA * NB)
    own = z * (NA * NB) + a * NB + b

    barrier = pltpu.get_barrier_semaphore()
    peers = [(k, c) for c in z_peer + a_peer + b_peer + [up, down]] + [(1 - k, chan)]
    for peer in peers:
        pl.semaphore_signal(barrier, inc=1, device_id=peer, device_id_type=MESH)
    pl.semaphore_wait(barrier, len(peers))

    slot = [0]

    def start(src, dst, peer):
        i = slot[0]
        slot[0] += 1
        copy = pltpu.make_async_remote_copy(
            src_ref=src, dst_ref=dst, send_sem=send.at[i], recv_sem=recv.at[i],
            device_id=peer, device_id_type=MESH,
        )
        copy.start()
        return copy

    sent = []

    def arrive(copies):
        for copy in copies:
            copy.wait_recv()
        sent.extend(copies)

    partner = (1 - k, chan)
    whole = pool.reshape(2, NZ, NA, NB, ROWS, 128)

    core = start(picked.at[pl.ds((1 - k) * (REFS // 2), REFS // 2)], core_in, partner)
    mine = pltpu.make_async_copy(export, pool.at[pl.ds(k * CH + own, 1)], core_send)
    mine.start()
    pool_z = [start(export, pool.at[pl.ds(k * CH + own, 1)], (k, c)) for c in z_peer]
    halos = [
        start(white.at[pl.ds(CH - HALO, HALO)], halo.at[0], (k, up)),
        start(white.at[pl.ds(0, HALO)], halo.at[1], (k, down)),
    ]

    arrive([core])
    half[...] = picked[pl.ds(k * (REFS // 2), REFS // 2)] + core_in[...]
    a_rs = [
        start(half.at[pl.ds(((a + j) % NA) * 8, 8)], a_in.at[j - 1], (k, a_peer[j - 1]))
        for j in range(1, NA)
    ]

    mine.wait()
    arrive(pool_z)
    column = whole.at[k, :, a, b]
    pool_a = [start(column, column, (k, c)) for c in a_peer]
    pool_c = [start(column, column, partner)]

    arrive(a_rs)
    a_sum[...] = half[pl.ds(a * 8, 8)] + a_in[0] + a_in[1] + a_in[2]
    b_rs = [
        start(a_sum.at[pl.ds(((b + j) % NB) * 2, 2)], b_in.at[j - 1], (k, b_peer[j - 1]))
        for j in range(1, NB)
    ]

    arrive(pool_a)
    plane = whole.at[k, :, :, b]
    pool_b = [start(plane, plane, (k, b_peer[0])), start(plane, plane, (k, b_peer[2]))]
    for j in range(1, NA):
        got = whole.at[k, :, (a + NA - j) % NA, b]
        pool_c.append(start(got, got, partner))

    arrive(b_rs)
    b_sum[...] = a_sum[pl.ds(b * 2, 2)] + b_in[0] + b_in[1] + b_in[2]
    z_rs = [start(b_sum, z_in.at[j - 1], (k, z_peer[j - 1])) for j in range(1, NZ)]

    arrive(z_rs)
    total = b_sum[...]
    for j in range(NZ - 1):
        total = total + z_in[j]
    lead = k * (REFS // 2) + a * 8
    pair = refs.at[pl.ds(lead + b * 2, 2)]
    refs[pl.ds(lead + b * 2, 2)] = total
    refs_b = [start(pair, pair, (k, c)) for c in b_peer]

    arrive(pool_b)
    low = whole.at[k, pl.ds(0, NZ // 2), :, (b + NB - 1) % NB]
    high = whole.at[k, pl.ds(NZ // 2, NZ // 2), :, (b + 1) % NB]
    pool_r = [start(low, low, (k, b_peer[0])), start(high, high, (k, b_peer[2]))]
    for c in ((b + NB - 1) % NB, (b + 1) % NB):
        got = whole.at[k, :, :, c]
        pool_c.append(start(got, got, partner))

    arrive(refs_b)
    eight = refs.at[pl.ds(lead, 8)]
    refs_a = [start(eight, eight, (k, c)) for c in a_peer]
    refs_c = [start(eight, eight, partner)]

    arrive(refs_a)
    for j in range(1, NA):
        got = refs.at[pl.ds(k * (REFS // 2) + ((a + NA - j) % NA) * 8, 8)]
        refs_c.append(start(got, got, partner))
    arrive(pool_r)
    got = whole.at[k, :, :, (b + 2) % NB]
    pool_c.append(start(got, got, partner))

    arrive(halos)
    arrive(pool_c)
    arrive(refs_c)
    for copy in sent:
        copy.wait_send()


def exchange(white, export, picked):
    vmem = pl.BlockSpec(memory_space=pltpu.VMEM)
    copies = 1 + 7 + 2 + 3 + 3 + 1 + 3 + 2 + 3 + 7 + 3 + 2 + 2 + 3 + 1 + 3 + 1
    return pl.pallas_call(
        exchange_kernel,
        name="exchange",
        in_specs=[vmem] * 3,
        out_specs=[vmem] * 3,
        out_shape=[
            jax.ShapeDtypeStruct((2, HALO, ROWS, 128), BF),
            jax.ShapeDtypeStruct((2 * CH, ROWS, 128), BF),
            jax.ShapeDtypeStruct((REFS, ROWS, 128), BF),
        ],
        scratch_shapes=[
            pltpu.VMEM((REFS // 2, ROWS, 128), BF),
            pltpu.VMEM((REFS // 2, ROWS, 128), BF),
            pltpu.VMEM((NA - 1, 8, ROWS, 128), BF),
            pltpu.VMEM((8, ROWS, 128), BF),
            pltpu.VMEM((NB - 1, 2, ROWS, 128), BF),
            pltpu.VMEM((2, ROWS, 128), BF),
            pltpu.VMEM((NZ - 1, 2, ROWS, 128), BF),
            pltpu.SemaphoreType.DMA((copies,)),
            pltpu.SemaphoreType.DMA((copies,)),
            pltpu.SemaphoreType.DMA,
            pltpu.SemaphoreType.DMA,
        ],
        compiler_params=pltpu.CompilerParams(
            collective_id=0, has_side_effects=True, vmem_limit_bytes=40 << 20
        ),
    )(white, export, picked)


def correlate_kernel(
    near, cross, mask, white, halo, pool_hbm, refs_hbm, table, out,
    ext, pool, refs, wide, right, left, x, sem,
):
    step = pl.program_id(0)
    base = (lax.axis_index("fibre") * (NZ * NA * NB) + lax.axis_index("chan")) * CH

    @pl.when(step == 0)
    def _():
        copies = [
            pltpu.make_async_copy(refs_hbm, refs, sem.at[0]),
            pltpu.make_async_copy(white, ext.at[pl.ds(HALO, CH)], sem.at[1]),
            pltpu.make_async_copy(halo.at[0], ext.at[pl.ds(0, HALO)], sem.at[2]),
            pltpu.make_async_copy(halo.at[1], ext.at[pl.ds(HALO + CH, HALO)], sem.at[3]),
            pltpu.make_async_copy(pool_hbm, pool, sem.at[4]),
        ]
        for copy in copies:
            copy.start()
        copies[0].wait()
        wide[...] = refs[...].astype(F32).reshape(REFS * ROWS, 128)
        for row in range(ROWS):
            right[row] = wide[pl.ds(row, REFS, stride=ROWS), :].astype(BF)
        for copy in copies[1:]:
            copy.wait()

    for c in range(GROUP):
        chan = step * GROUP + c
        total = ext[HALO + chan].astype(F32)
        for n in range(NN):
            total = total + ext[near[chan, n] - base + HALO].astype(F32)
        count = 1.0 + NN
        for j in range(XN):
            p = cross[chan, j]
            swapped = (p & ~15) | ((p & 3) << 2) | ((p >> 2) & 3)
            live = mask[chan, j].astype(F32)
            total = total + pool[jnp.where(p < CH, p, swapped)].astype(F32) * live
            count = count + live
        left[c] = (total / count).astype(BF).astype(F32)

    for c in range(GROUP):
        for t in range(4):
            lhs = [
                jnp.broadcast_to(left[c, row : row + 1, :], (16, 128)).astype(BF)
                for row in range(t, ROWS, 4)
            ]
            for r in range(0, REFS, 16):
                rhs = [right[row, r : r + 16, :] for row in range(t, ROWS, 4)]
                p = [u * v for u, v in zip(lhs, rhs)]
                q = [
                    lhs[2 * s + 1] * rhs[2 * s] - lhs[2 * s] * rhs[2 * s + 1]
                    for s in range(SEGS)
                ]
                g = ((p[0] + p[1]) + (p[2] + p[3])) + ((p[4] + p[5]) + (p[6] + p[7]))
                h = (q[0] + q[1]) + (q[2] + q[3])
                lo = c * REFS + r
                x[lo : lo + 16, t * 128 : t * 128 + 128] = g
                x[lo : lo + 16, 512 + t * 128 : 512 + t * 128 + 128] = h
    y = jnp.dot(x[...], table[...], preferred_element_type=F32)
    out[...] = y.astype(BF).reshape(GROUP, REFS, LAGS)


def correlate(near_ids, cross_ids, cross_mask, white, halo, pool, refs):
    smem = pl.BlockSpec(memory_space=pltpu.SMEM)
    hbm = pl.BlockSpec(memory_space=pl.ANY)
    return pl.pallas_call(
        correlate_kernel,
        name="correlate",
        grid=(CH // GROUP,),
        in_specs=[smem, smem, smem, hbm, hbm, hbm, hbm, pl.BlockSpec((SEG, LAGS), lambda i: (0, 0))],
        out_specs=pl.BlockSpec((GROUP, REFS, LAGS), lambda i: (i, 0, 0)),
        out_shape=jax.ShapeDtypeStruct((CH, REFS, LAGS), BF),
        scratch_shapes=[
            pltpu.VMEM((CH + 2 * HALO, ROWS, 128), BF),
            pltpu.VMEM((2 * CH, ROWS, 128), BF),
            pltpu.VMEM((REFS, ROWS, 128), BF),
            pltpu.VMEM((REFS * ROWS, 128), F32),
            pltpu.VMEM((ROWS, REFS, 128), BF),
            pltpu.VMEM((GROUP, ROWS, 128), F32),
            pltpu.VMEM((GROUP * REFS, SEG), BF),
            pltpu.SemaphoreType.DMA((5,)),
        ],
        compiler_params=pltpu.CompilerParams(vmem_limit_bytes=40 << 20),
    )(near_ids, cross_ids, cross_mask, white, halo, pool, refs, jnp.asarray(lag_table()))


def per_device(raw, starts, ref_ids, near_ids, cross_ids, cross_mask, export_loc):
    white, export, picked = spectra(starts, ref_ids, export_loc, raw)
    halo, pool, refs = exchange(white, export, picked)
    return correlate(near_ids, cross_ids, cross_mask, white, halo, pool, refs)


def solution(mesh):
    split = ("fibre", "chan")
    in_specs = (P(split, None), P(), P(), P(split, None), P(split, None), P(split, None), P(split))
    return jax.shard_map(
        per_device, mesh=mesh, in_specs=in_specs, out_specs=P(split, None, None), check_vma=False
    )
```

```python
import functools

import jax
import jax.numpy as jnp
import numpy as np
from jax import lax
from jax.experimental import pallas as pl
from jax.experimental.pallas import tpu as pltpu
from jax.sharding import PartitionSpec as P

SEG = 1024
SEGS = 4
REFS = 64
LAGS = 512
NN = 8
XN = 2
HALO = 16
CH = 128
NZ, NA, NB = 8, 4, 4
ROWS = SEGS * SEG // 128
GROUP = 16
MESH = pl.DeviceIdType.MESH
BF = jnp.bfloat16
F32 = jnp.float32


def forward_table():
    phase = (np.arange(SEG)[:, None] * np.arange(SEG // 2)[None, :]) % SEG
    theta = phase * (2.0 * np.pi / SEG)
    keep = (np.arange(SEG // 2) > 0)[None, :]
    return np.concatenate([np.cos(theta) * keep, -np.sin(theta)], 1).astype(BF)


def lag_table():
    phase = (np.arange(SEG // 2)[:, None] * (np.arange(LAGS) - LAGS // 2)[None, :]) % SEG
    theta = phase * (2.0 * np.pi / SEG)
    scale = 1.0 / np.sqrt(SEG // 2)
    table = np.concatenate([np.cos(theta) * scale, -np.sin(theta) * scale], 0).astype(BF)
    return (table.astype(np.float32) / SEGS).astype(BF)


def spectra_kernel(ints_in, raw, table_in, white, export, picked, ints, samples, table, seg, wide, load):
    base = (lax.axis_index("fibre") * (NZ * NA * NB) + lax.axis_index("chan")) * CH
    loads = [
        pltpu.make_async_copy(raw, samples.at[:, pl.ds(0, SEGS * SEG)], load.at[0]),
        pltpu.make_async_copy(ints_in, ints, load.at[1]),
        pltpu.make_async_copy(table_in, table, load.at[2]),
    ]
    for copy in loads:
        copy.start()
    samples[:, SEGS * SEG :] = jnp.zeros((CH, 128), BF)
    loads[0].wait()
    loads[1].wait()
    for s in range(SEGS):
        begin = ints[REFS + s]
        lead = pl.multiple_of((begin // 128) * 128, 128)
        window = samples[:, pl.ds(lead, SEG + 128)].astype(F32)
        cut = pltpu.roll(window, (SEG + 128) - (begin - lead), 1)[:, :SEG]
        seg[s * CH : (s + 1) * CH, :] = cut.astype(BF)
    loads[2].wait()
    for s in range(SEGS):
        spectrum = jnp.dot(
            seg[s * CH : (s + 1) * CH, :], table[...], preferred_element_type=F32
        )
        power = jnp.sum(spectrum * spectrum, -1, keepdims=True) / (SEG // 2)
        spectrum = spectrum / jnp.sqrt(power + 1e-06)
        for j in range(SEG // 128):
            wide[pl.ds(s * 8 + j, CH, stride=ROWS), :] = spectrum[:, j * 128 : (j + 1) * 128]

    def rows(channel):
        first = pl.multiple_of(channel * ROWS, ROWS)
        return wide[pl.ds(first, ROWS), :]

    def pick(r, carry):
        local = ints[r] - base
        mine = ((local >= 0) & (local < CH)).astype(F32)
        picked[r] = (rows(jnp.clip(local, 0, CH - 1)) * mine).astype(BF)
        return carry

    lax.fori_loop(0, REFS, pick, 0, unroll=8)
    export[0] = rows(ints[REFS + SEGS]).astype(BF)
    white[...] = wide[...].reshape(CH, ROWS, 128).astype(BF)


def spectra(ref_ids, starts, export_loc, raw):
    vmem = pl.BlockSpec(memory_space=pltpu.VMEM)
    hbm = pl.BlockSpec(memory_space=pl.ANY)
    fill = jnp.zeros((128 - REFS - SEGS - 1,), jnp.int32)
    ints = jnp.concatenate([ref_ids, starts, export_loc, fill])
    return pl.pallas_call(
        spectra_kernel,
        name="spectra",
        in_specs=[hbm] * 3,
        out_specs=[vmem] * 3,
        out_shape=[
            jax.ShapeDtypeStruct((CH, ROWS, 128), BF),
            jax.ShapeDtypeStruct((1, ROWS, 128), BF),
            jax.ShapeDtypeStruct((REFS, ROWS, 128), BF),
        ],
        scratch_shapes=[
            pltpu.SMEM((128,), jnp.int32),
            pltpu.VMEM((CH, SEGS * SEG + 128), BF),
            pltpu.VMEM((SEG, SEG), BF),
            pltpu.VMEM((CH * SEGS, SEG), BF),
            pltpu.VMEM((CH * ROWS, 128), F32),
            pltpu.SemaphoreType.DMA((3,)),
        ],
        compiler_params=pltpu.CompilerParams(vmem_limit_bytes=16 << 20),
    )(
        ints,
        pltpu.with_memory_space_constraint(raw, pltpu.HBM),
        pltpu.with_memory_space_constraint(jnp.asarray(forward_table()), pltpu.HBM),
    )


def exchange_kernel(
    white, export, picked, ext, pool, refs,
    core_in, half, a_in, a_sum, b_in, b_sum, z_in, send, recv,
):
    k = lax.axis_index("fibre")
    chan = lax.axis_index("chan")
    z, x, y = chan // (NA * NB), (chan // NB) % NA, chan % NB
    a = x * (1 - k) + y * k
    b = y * (1 - k) + x * k

    def at(zz, aa, bb):
        return zz * (NA * NB) + (aa * NB + bb) * (1 - k) + (bb * NB + aa) * k

    z_peer = [at((z + j) % NZ, a, b) for j in range(1, NZ)]
    a_peer = [at(z, (a + j) % NA, b) for j in range(1, NA)]
    b_peer = [at(z, a, (b + j) % NB) for j in range(1, NB)]
    up = (chan + 1) % (NZ * NA * NB)
    down = (chan + (NZ * NA * NB) - 1) % (NZ * NA * NB)
    own = z * (NA * NB) + a * NB + b

    barrier = pltpu.get_barrier_semaphore()
    peers = [(k, c) for c in z_peer + a_peer + b_peer + [up, down]] + [(1 - k, chan)]
    for peer in peers:
        pl.semaphore_signal(barrier, inc=1, device_id=peer, device_id_type=MESH)

    slot = [0]

    def start(src, dst, peer):
        i = slot[0]
        slot[0] += 1
        copy = pltpu.make_async_remote_copy(
            src_ref=src, dst_ref=dst, send_sem=send.at[i], recv_sem=recv.at[i],
            device_id=peer, device_id_type=MESH,
        )
        copy.start()
        return copy

    sent = []

    def arrive(copies):
        for copy in copies:
            copy.wait_recv()
        sent.extend(copies)

    partner = (1 - k, chan)
    whole = pool.reshape(2, NZ, NA, NB, ROWS, 128)

    pool[pl.ds(k * CH + own, 1)] = export[...]
    pl.semaphore_wait(barrier, len(peers))
    core = start(picked.at[pl.ds((1 - k) * (REFS // 2), REFS // 2)], core_in, partner)
    mine = pool.at[pl.ds(k * CH + own, 1)]
    pool_z = [start(export, mine, (k, c)) for c in z_peer]
    halos = [
        start(white.at[pl.ds(CH - HALO, HALO)], ext.at[pl.ds(0, HALO)], (k, up)),
        start(white.at[pl.ds(0, HALO)], ext.at[pl.ds(HALO + CH, HALO)], (k, down)),
    ]

    arrive([core])
    half[...] = picked[pl.ds(k * (REFS // 2), REFS // 2)] + core_in[...]
    a_rs = [
        start(half.at[pl.ds(((a + j) % NA) * 8, 8)], a_in.at[j - 1], (k, a_peer[j - 1]))
        for j in range(1, NA)
    ]

    arrive(pool_z)
    column = whole.at[k, :, a, b]
    pool_a = [start(column, column, (k, c)) for c in a_peer]
    pool_c = [start(column, column, partner)]
    ext[HALO : HALO + CH] = white[...]

    arrive(a_rs)
    a_sum[...] = half[pl.ds(a * 8, 8)] + a_in[0] + a_in[1] + a_in[2]
    b_rs = [
        start(a_sum.at[pl.ds(((b + j) % NB) * 2, 2)], b_in.at[j - 1], (k, b_peer[j - 1]))
        for j in range(1, NB)
    ]

    arrive(b_rs)
    b_sum[...] = a_sum[pl.ds(b * 2, 2)] + b_in[0] + b_in[1] + b_in[2]
    z_rs = [start(b_sum, z_in.at[j - 1], (k, z_peer[j - 1])) for j in range(1, NZ)]

    arrive(pool_a)
    plane = whole.at[k, :, :, b]
    pool_b = [start(plane, plane, (k, b_peer[0])), start(plane, plane, (k, b_peer[2]))]
    for j in range(1, NA):
        got = whole.at[k, :, (a + NA - j) % NA, b]
        pool_c.append(start(got, got, partner))

    arrive(z_rs)
    total = b_sum[...]
    for j in range(NZ - 1):
        total = total + z_in[j]
    lead = k * (REFS // 2) + a * 8
    pair = refs.at[pl.ds(lead + b * 2, 2)]
    refs[pl.ds(lead + b * 2, 2)] = total
    refs_b = [start(pair, pair, (k, c)) for c in b_peer]

    arrive(pool_b)
    low = whole.at[k, pl.ds(0, NZ // 2), :, (b + NB - 1) % NB]
    high = whole.at[k, pl.ds(NZ // 2, NZ // 2), :, (b + 1) % NB]
    pool_r = [start(low, low, (k, b_peer[0])), start(high, high, (k, b_peer[2]))]

    arrive(refs_b)
    eight = refs.at[pl.ds(lead, 8)]
    refs_a = [start(eight, eight, (k, c)) for c in a_peer]
    refs_c = [start(eight, eight, partner)]
    for c in ((b + NB - 1) % NB, (b + 1) % NB):
        got = whole.at[k, :, :, c]
        pool_c.append(start(got, got, partner))

    arrive(pool_r)
    got = whole.at[k, :, :, (b + 2) % NB]
    pool_c.append(start(got, got, partner))

    for j in range(1, NA):
        arrive([refs_a[j - 1]])
        got = refs.at[pl.ds(k * (REFS // 2) + ((a + NA - j) % NA) * 8, 8)]
        refs_c.append(start(got, got, partner))

    arrive(halos)
    arrive(pool_c)
    arrive(refs_c)
    for copy in sent:
        copy.wait_send()


def exchange(white, export, picked):
    vmem = pl.BlockSpec(memory_space=pltpu.VMEM)
    copies = 1 + 3 + 7 + 3 + 2 + 7 + 3 + 1 + 3 + 2 + 3 + 3 + 1 + 2 + 2 + 3 + 1
    return pl.pallas_call(
        exchange_kernel,
        name="exchange",
        in_specs=[vmem] * 3,
        out_specs=[vmem] * 3,
        out_shape=[
            jax.ShapeDtypeStruct((CH + 2 * HALO, ROWS, 128), BF),
            jax.ShapeDtypeStruct((2 * CH, ROWS, 128), BF),
            jax.ShapeDtypeStruct((REFS, ROWS, 128), BF),
        ],
        scratch_shapes=[
            pltpu.VMEM((REFS // 2, ROWS, 128), BF),
            pltpu.VMEM((REFS // 2, ROWS, 128), BF),
            pltpu.VMEM((NA - 1, 8, ROWS, 128), BF),
            pltpu.VMEM((8, ROWS, 128), BF),
            pltpu.VMEM((NB - 1, 2, ROWS, 128), BF),
            pltpu.VMEM((2, ROWS, 128), BF),
            pltpu.VMEM((NZ - 1, 2, ROWS, 128), BF),
            pltpu.SemaphoreType.DMA((copies,)),
            pltpu.SemaphoreType.DMA((copies,)),
        ],
        compiler_params=pltpu.CompilerParams(
            collective_id=0, has_side_effects=True, vmem_limit_bytes=24 << 20
        ),
    )(white, export, picked)


def correlate_kernel(
    near_in, cross_in, mask_in, ext, pool, refs, table, out,
    near, cross, mask, wide, right, left, x, rows, load, store,
):
    base = (lax.axis_index("fibre") * (NZ * NA * NB) + lax.axis_index("chan")) * CH
    loads = [
        pltpu.make_async_copy(near_in, near, load.at[0]),
        pltpu.make_async_copy(cross_in, cross, load.at[1]),
        pltpu.make_async_copy(mask_in, mask, load.at[2]),
    ]
    for copy in loads:
        copy.start()
    wide[...] = refs[...].astype(F32).reshape(REFS * ROWS, 128)
    for row in range(ROWS):
        right[row] = wide[pl.ds(row, REFS, stride=ROWS), :].astype(BF)
    for copy in loads:
        copy.wait()
    steps = CH // GROUP

    def put(step):
        return pltpu.make_async_copy(
            rows.at[step % 2], out.at[pl.ds(step * GROUP, GROUP)], store.at[step % 2]
        )

    def body(step, carry):
        for c in range(GROUP):
            chan = step * GROUP + c
            total = ext[HALO + chan].astype(F32)
            for n in range(NN):
                total = total + ext[near[n, chan] - base + HALO].astype(F32)
            count = 1.0 + NN
            for j in range(XN):
                p = cross[j, chan]
                swapped = (p & ~15) | ((p & 3) << 2) | ((p >> 2) & 3)
                live = mask[j, chan].astype(F32)
                total = total + pool[jnp.where(p < CH, p, swapped)].astype(F32) * live
                count = count + live
            left[c] = (total / count).astype(BF).astype(F32)

        for c in range(GROUP):
            for t in range(4):
                lhs = [
                    jnp.broadcast_to(left[c, row : row + 1, :], (16, 128)).astype(BF)
                    for row in range(t, ROWS, 4)
                ]
                for r in range(0, REFS, 16):
                    rhs = [right[row, r : r + 16, :] for row in range(t, ROWS, 4)]
                    p = [u * v for u, v in zip(lhs, rhs)]
                    q = [
                        lhs[2 * s + 1] * rhs[2 * s] - lhs[2 * s] * rhs[2 * s + 1]
                        for s in range(SEGS)
                    ]
                    g = ((p[0] + p[1]) + (p[2] + p[3])) + ((p[4] + p[5]) + (p[6] + p[7]))
                    h = (q[0] + q[1]) + (q[2] + q[3])
                    lo = c * REFS + r
                    x[lo : lo + 16, t * 128 : t * 128 + 128] = g
                    x[lo : lo + 16, 512 + t * 128 : 512 + t * 128 + 128] = h

        @pl.when(step >= 2)
        def _():
            put(step - 2).wait()

        y = jnp.dot(x[...], table[...], preferred_element_type=F32)
        rows[step % 2] = y.astype(BF).reshape(GROUP, REFS, LAGS)
        put(step).start()
        return carry

    lax.fori_loop(0, steps, body, 0)
    put(steps - 2).wait()
    put(steps - 1).wait()


def correlate(near_ids, cross_ids, cross_mask, ext, pool, refs):
    vmem = pl.BlockSpec(memory_space=pltpu.VMEM)
    hbm = pl.BlockSpec(memory_space=pl.ANY)
    return pl.pallas_call(
        correlate_kernel,
        name="correlate",
        in_specs=[hbm] * 3 + [vmem] * 4,
        out_specs=hbm,
        out_shape=jax.ShapeDtypeStruct((CH, REFS, LAGS), BF),
        scratch_shapes=[
            pltpu.SMEM((NN, CH), jnp.int32),
            pltpu.SMEM((XN, CH), jnp.int32),
            pltpu.SMEM((XN, CH), jnp.int32),
            pltpu.VMEM((REFS * ROWS, 128), F32),
            pltpu.VMEM((ROWS, REFS, 128), BF),
            pltpu.VMEM((GROUP, ROWS, 128), F32),
            pltpu.VMEM((GROUP * REFS, SEG), BF),
            pltpu.VMEM((2, GROUP, REFS, LAGS), BF),
            pltpu.SemaphoreType.DMA((3,)),
            pltpu.SemaphoreType.DMA((2,)),
        ],
        compiler_params=pltpu.CompilerParams(vmem_limit_bytes=24 << 20),
    )(near_ids.T, cross_ids.T, cross_mask.T, ext, pool, refs, jnp.asarray(lag_table()))


def per_device(raw, starts, ref_ids, near_ids, cross_ids, cross_mask, export_loc):
    white, export, picked = spectra(ref_ids, starts, export_loc, raw)
    ext, pool, refs = exchange(white, export, picked)
    return correlate(near_ids, cross_ids, cross_mask, ext, pool, refs)


def solution(mesh):
    split = ("fibre", "chan")
    in_specs = (P(split, None), P(), P(), P(split, None), P(split, None), P(split, None), P(split))
    return jax.shard_map(
        per_device, mesh=mesh, in_specs=in_specs, out_specs=P(split, None, None), check_vma=False
    )
```

```python
import functools

import jax
import jax.numpy as jnp
import numpy as np
from jax import lax
from jax.experimental import pallas as pl
from jax.experimental.pallas import tpu as pltpu
from jax.sharding import PartitionSpec as P

SEG = 1024
SEGS = 4
REFS = 64
LAGS = 512
NN = 8
XN = 2
HALO = 16
CH = 128
NZ, NA, NB = 8, 4, 4
ROWS = SEGS * SEG // 128
GROUP = 16
HALF = 8
MESH = pl.DeviceIdType.MESH
BF = jnp.bfloat16
F32 = jnp.float32


def forward_table():
    phase = (np.arange(SEG)[:, None] * np.arange(SEG // 2)[None, :]) % SEG
    theta = phase * (2.0 * np.pi / SEG)
    keep = (np.arange(SEG // 2) > 0)[None, :]
    return np.concatenate([np.cos(theta) * keep, -np.sin(theta)], 1).astype(BF)


def lag_table():
    phase = (np.arange(SEG // 2)[:, None] * (np.arange(LAGS) - LAGS // 2)[None, :]) % SEG
    theta = phase * (2.0 * np.pi / SEG)
    scale = 1.0 / np.sqrt(SEG // 2)
    table = np.concatenate([np.cos(theta) * scale, -np.sin(theta) * scale], 0).astype(BF)
    return (table.astype(np.float32) / SEGS).astype(BF)


def spectra_kernel(ints_in, raw, table_in, white, export, picked, ints, samples, table, seg, wide, load):
    base = (lax.axis_index("fibre") * (NZ * NA * NB) + lax.axis_index("chan")) * CH
    loads = [
        pltpu.make_async_copy(raw, samples.at[:, pl.ds(0, SEGS * SEG)], load.at[0]),
        pltpu.make_async_copy(ints_in, ints, load.at[1]),
        pltpu.make_async_copy(table_in, table, load.at[2]),
    ]
    for copy in loads:
        copy.start()
    samples[:, SEGS * SEG :] = jnp.zeros((CH, 128), BF)
    loads[0].wait()
    loads[1].wait()
    for s in range(SEGS):
        begin = ints[REFS + s]
        lead = pl.multiple_of((begin // 128) * 128, 128)
        window = samples[:, pl.ds(lead, SEG + 128)].astype(F32)
        cut = pltpu.roll(window, (SEG + 128) - (begin - lead), 1)[:, :SEG]
        seg[s * CH : (s + 1) * CH, :] = cut.astype(BF)
    loads[2].wait()
    for s in range(SEGS):
        spectrum = jnp.dot(
            seg[s * CH : (s + 1) * CH, :], table[...], preferred_element_type=F32
        )
        power = jnp.sum(spectrum * spectrum, -1, keepdims=True) / (SEG // 2)
        spectrum = spectrum / jnp.sqrt(power + 1e-06)
        for j in range(SEG // 128):
            wide[pl.ds(s * 8 + j, CH, stride=ROWS), :] = spectrum[:, j * 128 : (j + 1) * 128]

    def rows(channel):
        first = pl.multiple_of(channel * ROWS, ROWS)
        return wide[pl.ds(first, ROWS), :]

    def pick(r, carry):
        local = ints[r] - base
        mine = ((local >= 0) & (local < CH)).astype(F32)
        picked[r] = (rows(jnp.clip(local, 0, CH - 1)) * mine).astype(BF)
        return carry

    lax.fori_loop(0, REFS, pick, 0, unroll=8)
    export[0] = rows(ints[REFS + SEGS]).astype(BF)
    white[...] = wide[...].reshape(CH, ROWS, 128).astype(BF)


def spectra(ref_ids, starts, export_loc, raw):
    vmem = pl.BlockSpec(memory_space=pltpu.VMEM)
    hbm = pl.BlockSpec(memory_space=pl.ANY)
    fill = jnp.zeros((128 - REFS - SEGS - 1,), jnp.int32)
    ints = jnp.concatenate([ref_ids, starts, export_loc, fill])
    return pl.pallas_call(
        spectra_kernel,
        name="spectra",
        in_specs=[hbm] * 3,
        out_specs=[vmem] * 3,
        out_shape=[
            jax.ShapeDtypeStruct((CH, ROWS, 128), BF),
            jax.ShapeDtypeStruct((1, ROWS, 128), BF),
            jax.ShapeDtypeStruct((REFS, ROWS, 128), BF),
        ],
        scratch_shapes=[
            pltpu.SMEM((128,), jnp.int32),
            pltpu.VMEM((CH, SEGS * SEG + 128), BF),
            pltpu.VMEM((SEG, SEG), BF),
            pltpu.VMEM((CH * SEGS, SEG), BF),
            pltpu.VMEM((CH * ROWS, 128), F32),
            pltpu.SemaphoreType.DMA((3,)),
        ],
        compiler_params=pltpu.CompilerParams(vmem_limit_bytes=16 << 20),
    )(
        ints,
        pltpu.with_memory_space_constraint(raw, pltpu.HBM),
        pltpu.with_memory_space_constraint(jnp.asarray(forward_table()), pltpu.HBM),
    )


def exchange_kernel(
    white, export, picked, ext, pool, refs,
    core_in, half, a_in, a_sum, b_in, b_sum, z_in, send, recv,
):
    k = lax.axis_index("fibre")
    chan = lax.axis_index("chan")
    z, x, y = chan // (NA * NB), (chan // NB) % NA, chan % NB
    a = x * (1 - k) + y * k
    b = y * (1 - k) + x * k

    def at(zz, aa, bb):
        return zz * (NA * NB) + (aa * NB + bb) * (1 - k) + (bb * NB + aa) * k

    z_peer = [at((z + j) % NZ, a, b) for j in range(1, NZ)]
    a_peer = [at(z, (a + j) % NA, b) for j in range(1, NA)]
    b_peer = [at(z, a, (b + j) % NB) for j in range(1, NB)]
    up = (chan + 1) % (NZ * NA * NB)
    down = (chan + (NZ * NA * NB) - 1) % (NZ * NA * NB)
    own = z * (NA * NB) + a * NB + b

    barrier = pltpu.get_barrier_semaphore()
    peers = [(k, c) for c in z_peer + a_peer + b_peer + [up, down]] + [(1 - k, chan)]
    for peer in peers:
        pl.semaphore_signal(barrier, inc=1, device_id=peer, device_id_type=MESH)

    slot = [0]

    def start(src, dst, peer):
        i = slot[0]
        slot[0] += 1
        copy = pltpu.make_async_remote_copy(
            src_ref=src, dst_ref=dst, send_sem=send.at[i], recv_sem=recv.at[i],
            device_id=peer, device_id_type=MESH,
        )
        copy.start()
        return copy

    sent = []

    def arrive(copies):
        for copy in copies:
            copy.wait_recv()
        sent.extend(copies)

    partner = (1 - k, chan)
    whole = pool.reshape(2, NZ, NA, NB, ROWS, 128)

    pool[pl.ds(k * CH + own, 1)] = export[...]
    pl.semaphore_wait(barrier, len(peers))
    core = start(picked.at[pl.ds((1 - k) * (REFS // 2), REFS // 2)], core_in, partner)
    mine = pool.at[pl.ds(k * CH + own, 1)]
    pool_z = [start(export, mine, (k, c)) for c in z_peer]
    halos = [
        start(white.at[pl.ds(CH - HALO, HALO)], ext.at[pl.ds(0, HALO)], (k, up)),
        start(white.at[pl.ds(0, HALO)], ext.at[pl.ds(HALO + CH, HALO)], (k, down)),
    ]

    arrive([core])
    half[...] = picked[pl.ds(k * (REFS // 2), REFS // 2)] + core_in[...]
    a_rs = [
        start(half.at[pl.ds(((a + j) % NA) * 8, 8)], a_in.at[j - 1], (k, a_peer[j - 1]))
        for j in range(1, NA)
    ]

    arrive(pool_z)
    column = whole.at[k, :, a, b]
    pool_a = [start(column, column, (k, c)) for c in a_peer]
    pool_c = [start(column, column, partner)]
    ext[HALO : HALO + CH] = white[...]

    arrive(a_rs)
    a_sum[...] = half[pl.ds(a * 8, 8)] + a_in[0] + a_in[1] + a_in[2]
    b_rs = [
        start(a_sum.at[pl.ds(((b + j) % NB) * 2, 2)], b_in.at[j - 1], (k, b_peer[j - 1]))
        for j in range(1, NB)
    ]

    arrive(b_rs)
    b_sum[...] = a_sum[pl.ds(b * 2, 2)] + b_in[0] + b_in[1] + b_in[2]
    z_rs = [start(b_sum, z_in.at[j - 1], (k, z_peer[j - 1])) for j in range(1, NZ)]

    arrive(pool_a)
    plane = whole.at[k, :, :, b]
    pool_b = [start(plane, plane, (k, b_peer[0])), start(plane, plane, (k, b_peer[2]))]
    for j in range(1, NA):
        got = whole.at[k, :, (a + NA - j) % NA, b]
        pool_c.append(start(got, got, partner))

    arrive(z_rs)
    total = b_sum[...]
    for j in range(NZ - 1):
        total = total + z_in[j]
    lead = k * (REFS // 2) + a * 8
    pair = refs.at[pl.ds(lead + b * 2, 2)]
    refs[pl.ds(lead + b * 2, 2)] = total
    refs_b = [start(pair, pair, (k, c)) for c in b_peer]

    arrive(pool_b)
    low = whole.at[k, pl.ds(0, NZ // 2), :, (b + NB - 1) % NB]
    high = whole.at[k, pl.ds(NZ // 2, NZ // 2), :, (b + 1) % NB]
    pool_r = [start(low, low, (k, b_peer[0])), start(high, high, (k, b_peer[2]))]

    arrive(refs_b)
    eight = refs.at[pl.ds(lead, 8)]
    refs_a = [start(eight, eight, (k, c)) for c in a_peer]
    refs_c = [start(eight, eight, partner)]
    for c in ((b + NB - 1) % NB, (b + 1) % NB):
        got = whole.at[k, :, :, c]
        pool_c.append(start(got, got, partner))

    arrive(pool_r)
    got = whole.at[k, :, :, (b + 2) % NB]
    pool_c.append(start(got, got, partner))

    for j in range(1, NA):
        arrive([refs_a[j - 1]])
        got = refs.at[pl.ds(k * (REFS // 2) + ((a + NA - j) % NA) * 8, 8)]
        refs_c.append(start(got, got, partner))

    arrive(halos)
    arrive(pool_c)
    arrive(refs_c)
    for copy in sent:
        copy.wait_send()


def exchange(white, export, picked):
    vmem = pl.BlockSpec(memory_space=pltpu.VMEM)
    copies = 1 + 3 + 7 + 3 + 2 + 7 + 3 + 1 + 3 + 2 + 3 + 3 + 1 + 2 + 2 + 3 + 1
    return pl.pallas_call(
        exchange_kernel,
        name="exchange",
        in_specs=[vmem] * 3,
        out_specs=[vmem] * 3,
        out_shape=[
            jax.ShapeDtypeStruct((CH + 2 * HALO, ROWS, 128), BF),
            jax.ShapeDtypeStruct((2 * CH, ROWS, 128), BF),
            jax.ShapeDtypeStruct((REFS, ROWS, 128), BF),
        ],
        scratch_shapes=[
            pltpu.VMEM((REFS // 2, ROWS, 128), BF),
            pltpu.VMEM((REFS // 2, ROWS, 128), BF),
            pltpu.VMEM((NA - 1, 8, ROWS, 128), BF),
            pltpu.VMEM((8, ROWS, 128), BF),
            pltpu.VMEM((NB - 1, 2, ROWS, 128), BF),
            pltpu.VMEM((2, ROWS, 128), BF),
            pltpu.VMEM((NZ - 1, 2, ROWS, 128), BF),
            pltpu.SemaphoreType.DMA((copies,)),
            pltpu.SemaphoreType.DMA((copies,)),
        ],
        compiler_params=pltpu.CompilerParams(
            collective_id=0, has_side_effects=True, vmem_limit_bytes=24 << 20
        ),
    )(white, export, picked)


def products(left, right, c):
    low = [[None] * 4 for _ in range(REFS // 16)]
    high = [[None] * 4 for _ in range(REFS // 16)]
    for t in range(4):
        lhs = [
            jnp.broadcast_to(left[c, row : row + 1, :], (16, 128)).astype(BF)
            for row in range(t, ROWS, 4)
        ]
        for r in range(REFS // 16):
            rhs = [right[row, r * 16 : r * 16 + 16, :] for row in range(t, ROWS, 4)]
            p = [u * v for u, v in zip(lhs, rhs)]
            q = [lhs[2 * s + 1] * rhs[2 * s] - lhs[2 * s] * rhs[2 * s + 1] for s in range(SEGS)]
            low[r][t] = ((p[0] + p[1]) + (p[2] + p[3])) + ((p[4] + p[5]) + (p[6] + p[7]))
            high[r][t] = (q[0] + q[1]) + (q[2] + q[3])
    return jnp.concatenate([jnp.concatenate(low[r] + high[r], 1) for r in range(REFS // 16)], 0)


def correlate_kernel(
    near_in, cross_in, mask_in, ext, pool, refs, table, out,
    near, cross, mask, wide, right, left, rows, load, store,
):
    base = (lax.axis_index("fibre") * (NZ * NA * NB) + lax.axis_index("chan")) * CH
    loads = [
        pltpu.make_async_copy(near_in, near, load.at[0]),
        pltpu.make_async_copy(cross_in, cross, load.at[1]),
        pltpu.make_async_copy(mask_in, mask, load.at[2]),
    ]
    for copy in loads:
        copy.start()
    wide[...] = refs[...].astype(F32).reshape(REFS * ROWS, 128)
    for row in range(ROWS):
        right[row] = wide[pl.ds(row, REFS, stride=ROWS), :].astype(BF)
    for copy in loads:
        copy.wait()
    steps = CH // GROUP

    def put(step):
        return pltpu.make_async_copy(
            rows.at[step % 2], out.at[pl.ds(step * GROUP, GROUP)], store.at[step % 2]
        )

    def body(step, carry):
        for c in range(GROUP):
            chan = step * GROUP + c
            total = ext[HALO + chan].astype(F32)
            for n in range(NN):
                total = total + ext[near[n, chan] - base + HALO].astype(F32)
            links = 0
            for j in range(XN):
                p = cross[j, chan]
                swapped = (p & ~15) | ((p & 3) << 2) | ((p >> 2) & 3)
                live = mask[j, chan]
                total = total + pool[jnp.where(p < CH, p, swapped)].astype(F32) * live.astype(F32)
                links = links + live
            share = jnp.where(links == 0, 1.0 / 9, jnp.where(links == 1, 0.1, 1.0 / 11)).astype(F32)
            left[c] = (total * share).astype(BF).astype(F32)

        @pl.when(step >= 2)
        def _():
            put(step - 2).wait()

        cross_spectra = [
            jnp.concatenate([products(left, right, c) for c in range(h, h + HALF)], 0)
            for h in range(0, GROUP, HALF)
        ]
        for h, spectrum in enumerate(cross_spectra):
            y = jnp.dot(spectrum, table[...], preferred_element_type=F32)
            rows[step % 2, h * HALF : (h + 1) * HALF] = y.astype(BF).reshape(HALF, REFS, LAGS)
        put(step).start()
        return carry

    lax.fori_loop(0, steps, body, 0)
    put(steps - 2).wait()
    put(steps - 1).wait()


def correlate(near_ids, cross_ids, cross_mask, ext, pool, refs):
    vmem = pl.BlockSpec(memory_space=pltpu.VMEM)
    hbm = pl.BlockSpec(memory_space=pl.ANY)
    return pl.pallas_call(
        correlate_kernel,
        name="correlate",
        in_specs=[hbm] * 3 + [vmem] * 4,
        out_specs=hbm,
        out_shape=jax.ShapeDtypeStruct((CH, REFS, LAGS), BF),
        scratch_shapes=[
            pltpu.SMEM((NN, CH), jnp.int32),
            pltpu.SMEM((XN, CH), jnp.int32),
            pltpu.SMEM((XN, CH), jnp.int32),
            pltpu.VMEM((REFS * ROWS, 128), F32),
            pltpu.VMEM((ROWS, REFS, 128), BF),
            pltpu.VMEM((GROUP, ROWS, 128), F32),
            pltpu.VMEM((2, GROUP, REFS, LAGS), BF),
            pltpu.SemaphoreType.DMA((3,)),
            pltpu.SemaphoreType.DMA((2,)),
        ],
        compiler_params=pltpu.CompilerParams(vmem_limit_bytes=24 << 20),
    )(near_ids.T, cross_ids.T, cross_mask.T, ext, pool, refs, jnp.asarray(lag_table()))


def per_device(raw, starts, ref_ids, near_ids, cross_ids, cross_mask, export_loc):
    white, export, picked = spectra(ref_ids, starts, export_loc, raw)
    ext, pool, refs = exchange(white, export, picked)
    return correlate(near_ids, cross_ids, cross_mask, ext, pool, refs)


def solution(mesh):
    split = ("fibre", "chan")
    in_specs = (P(split, None), P(), P(), P(split, None), P(split, None), P(split, None), P(split))
    return jax.shard_map(
        per_device, mesh=mesh, in_specs=in_specs, out_specs=P(split, None, None), check_vma=False
    )
```

```python
import functools

import jax
import jax.numpy as jnp
import numpy as np
from jax import lax
from jax.experimental import pallas as pl
from jax.experimental.pallas import tpu as pltpu
from jax.sharding import PartitionSpec as P

SEG = 1024
SEGS = 4
REFS = 64
LAGS = 512
NN = 8
XN = 2
HALO = 16
CH = 128
NZ, NA, NB = 8, 4, 4
ROWS = SEGS * SEG // 128
GROUP = 16
HALF = 8
FAR_RING4 = (2, 1, 3)
FAR_RING8 = (4, 3, 5, 2, 6, 1, 7)
MESH = pl.DeviceIdType.MESH
BF = jnp.bfloat16
F32 = jnp.float32


def forward_table():
    phase = (np.arange(SEG)[:, None] * np.arange(SEG // 2)[None, :]) % SEG
    theta = phase * (2.0 * np.pi / SEG)
    keep = (np.arange(SEG // 2) > 0)[None, :]
    return np.concatenate([np.cos(theta) * keep, -np.sin(theta)], 1).astype(BF)


def lag_table():
    phase = (np.arange(SEG // 2)[:, None] * (np.arange(LAGS) - LAGS // 2)[None, :]) % SEG
    theta = phase * (2.0 * np.pi / SEG)
    scale = 1.0 / np.sqrt(SEG // 2)
    table = np.concatenate([np.cos(theta) * scale, -np.sin(theta) * scale], 0).astype(BF)
    return (table.astype(np.float32) / SEGS).astype(BF)


def spectra_kernel(ints_in, raw, table_in, white, export, picked, ints, samples, table, seg, wide, load):
    base = (lax.axis_index("fibre") * (NZ * NA * NB) + lax.axis_index("chan")) * CH
    loads = [
        pltpu.make_async_copy(raw, samples.at[:, pl.ds(0, SEGS * SEG)], load.at[0]),
        pltpu.make_async_copy(ints_in, ints, load.at[1]),
        pltpu.make_async_copy(table_in, table, load.at[2]),
    ]
    for copy in loads:
        copy.start()
    samples[:, SEGS * SEG :] = jnp.zeros((CH, 128), BF)
    loads[0].wait()
    loads[1].wait()
    for s in range(SEGS):
        begin = ints[REFS + s]
        lead = pl.multiple_of((begin // 128) * 128, 128)
        offset = begin - lead
        turned = [
            pltpu.roll(
                samples[:, pl.ds(lead + j * 128, 128)].astype(F32), (128 - offset) % 128, 1
            )
            for j in range(SEG // 128 + 1)
        ]
        here = lax.broadcasted_iota(jnp.int32, (CH, 128), 1) < 128 - offset
        for j in range(SEG // 128):
            cut = jnp.where(here, turned[j], turned[j + 1]).astype(BF)
            seg[s * CH : (s + 1) * CH, j * 128 : (j + 1) * 128] = cut
    loads[2].wait()
    for s in range(SEGS):
        spectrum = jnp.dot(
            seg[s * CH : (s + 1) * CH, :], table[...], preferred_element_type=F32
        )
        power = jnp.sum(spectrum * spectrum, -1, keepdims=True) / (SEG // 2)
        spectrum = spectrum / jnp.sqrt(power + 1e-06)
        for j in range(SEG // 128):
            wide[pl.ds(s * 8 + j, CH, stride=ROWS), :] = spectrum[:, j * 128 : (j + 1) * 128]

    def rows(channel):
        first = pl.multiple_of(channel * ROWS, ROWS)
        return wide[pl.ds(first, ROWS), :]

    def pick(r, carry):
        local = ints[r] - base
        mine = ((local >= 0) & (local < CH)).astype(F32)
        picked[r] = (rows(jnp.clip(local, 0, CH - 1)) * mine).astype(BF)
        return carry

    lax.fori_loop(0, REFS, pick, 0, unroll=8)
    export[0] = rows(ints[REFS + SEGS]).astype(BF)
    white[...] = wide[...].reshape(CH, ROWS, 128).astype(BF)


def spectra(ref_ids, starts, export_loc, raw):
    vmem = pl.BlockSpec(memory_space=pltpu.VMEM)
    hbm = pl.BlockSpec(memory_space=pl.ANY)
    fill = jnp.zeros((128 - REFS - SEGS - 1,), jnp.int32)
    ints = jnp.concatenate([ref_ids, starts, export_loc, fill])
    return pl.pallas_call(
        spectra_kernel,
        name="spectra",
        in_specs=[hbm] * 3,
        out_specs=[vmem] * 3,
        out_shape=[
            jax.ShapeDtypeStruct((CH, ROWS, 128), BF),
            jax.ShapeDtypeStruct((1, ROWS, 128), BF),
            jax.ShapeDtypeStruct((REFS, ROWS, 128), BF),
        ],
        scratch_shapes=[
            pltpu.SMEM((128,), jnp.int32),
            pltpu.VMEM((CH, SEGS * SEG + 128), BF),
            pltpu.VMEM((SEG, SEG), BF),
            pltpu.VMEM((CH * SEGS, SEG), BF),
            pltpu.VMEM((CH * ROWS, 128), F32),
            pltpu.SemaphoreType.DMA((3,)),
        ],
        compiler_params=pltpu.CompilerParams(vmem_limit_bytes=16 << 20),
    )(
        ints,
        pltpu.with_memory_space_constraint(raw, pltpu.HBM),
        pltpu.with_memory_space_constraint(jnp.asarray(forward_table()), pltpu.HBM),
    )


def exchange_kernel(
    white, export, picked, ext, pool, refs,
    core_in, half, a_in, a_sum, b_in, b_sum, z_in, send, recv,
):
    k = lax.axis_index("fibre")
    chan = lax.axis_index("chan")
    z, x, y = chan // (NA * NB), (chan // NB) % NA, chan % NB
    a = x * (1 - k) + y * k
    b = y * (1 - k) + x * k

    def at(zz, aa, bb):
        return zz * (NA * NB) + (aa * NB + bb) * (1 - k) + (bb * NB + aa) * k

    z_peer = [at((z + j) % NZ, a, b) for j in range(1, NZ)]
    a_peer = [at(z, (a + j) % NA, b) for j in range(1, NA)]
    b_peer = [at(z, a, (b + j) % NB) for j in range(1, NB)]
    up = (chan + 1) % (NZ * NA * NB)
    down = (chan + (NZ * NA * NB) - 1) % (NZ * NA * NB)
    own = z * (NA * NB) + a * NB + b

    barrier = pltpu.get_barrier_semaphore()
    peers = [(k, c) for c in z_peer + a_peer + b_peer + [up, down]] + [(1 - k, chan)]
    for peer in peers:
        pl.semaphore_signal(barrier, inc=1, device_id=peer, device_id_type=MESH)

    slot = [0]

    def start(src, dst, peer):
        i = slot[0]
        slot[0] += 1
        copy = pltpu.make_async_remote_copy(
            src_ref=src, dst_ref=dst, send_sem=send.at[i], recv_sem=recv.at[i],
            device_id=peer, device_id_type=MESH,
        )
        copy.start()
        return copy

    sent = []

    def arrive(copies):
        for copy in copies:
            copy.wait_recv()
        sent.extend(copies)

    partner = (1 - k, chan)
    whole = pool.at[pl.ds(0, 2 * CH)].reshape(2, NZ, NA, NB, ROWS, 128)

    pool[pl.ds(k * CH + own, 1)] = export[...]
    pool[pl.ds(2 * CH, 1)] = jnp.zeros((1, ROWS, 128), BF)
    pl.semaphore_wait(barrier, len(peers))
    core = start(picked.at[pl.ds((1 - k) * (REFS // 2), REFS // 2)], core_in, partner)
    mine = pool.at[pl.ds(k * CH + own, 1)]
    pool_z = [start(export, mine, (k, z_peer[j - 1])) for j in FAR_RING8]
    halos = [
        start(white.at[pl.ds(CH - HALO, HALO)], ext.at[pl.ds(0, HALO)], (k, up)),
        start(white.at[pl.ds(0, HALO)], ext.at[pl.ds(HALO + CH, HALO)], (k, down)),
    ]

    arrive([core])
    half[...] = picked[pl.ds(k * (REFS // 2), REFS // 2)] + core_in[...]
    a_rs = [
        start(half.at[pl.ds(((a + j) % NA) * 8, 8)], a_in.at[j - 1], (k, a_peer[j - 1]))
        for j in FAR_RING4
    ]

    arrive(pool_z)
    column = whole.at[k, :, a, b]
    pool_a = [start(column, column, (k, a_peer[j - 1])) for j in FAR_RING4]
    pool_c = [start(column, column, partner)]
    ext[HALO : HALO + CH] = white[...]

    arrive(a_rs)
    a_sum[...] = half[pl.ds(a * 8, 8)] + a_in[0] + a_in[1] + a_in[2]
    b_rs = [
        start(a_sum.at[pl.ds(((b + j) % NB) * 2, 2)], b_in.at[j - 1], (k, b_peer[j - 1]))
        for j in FAR_RING4
    ]

    arrive(b_rs)
    b_sum[...] = a_sum[pl.ds(b * 2, 2)] + b_in[0] + b_in[1] + b_in[2]
    z_rs = [start(b_sum, z_in.at[j - 1], (k, z_peer[j - 1])) for j in FAR_RING8]

    arrive(pool_a)
    plane = whole.at[k, :, :, b]
    pool_b = [start(plane, plane, (k, b_peer[0])), start(plane, plane, (k, b_peer[2]))]
    for j in range(1, NA):
        got = whole.at[k, :, (a + NA - j) % NA, b]
        pool_c.append(start(got, got, partner))

    arrive(z_rs)
    total = b_sum[...]
    for j in range(NZ - 1):
        total = total + z_in[j]
    lead = k * (REFS // 2) + a * 8
    pair = refs.at[pl.ds(lead + b * 2, 2)]
    refs[pl.ds(lead + b * 2, 2)] = total
    refs_b = [start(pair, pair, (k, b_peer[j - 1])) for j in FAR_RING4]

    arrive(pool_b)
    low = whole.at[k, pl.ds(0, NZ // 2), :, (b + NB - 1) % NB]
    high = whole.at[k, pl.ds(NZ // 2, NZ // 2), :, (b + 1) % NB]
    pool_r = [start(low, low, (k, b_peer[0])), start(high, high, (k, b_peer[2]))]

    arrive(refs_b)
    eight = refs.at[pl.ds(lead, 8)]
    refs_a = [start(eight, eight, (k, a_peer[j - 1])) for j in FAR_RING4]
    refs_c = [start(eight, eight, partner)]
    for c in ((b + NB - 1) % NB, (b + 1) % NB):
        got = whole.at[k, :, :, c]
        pool_c.append(start(got, got, partner))

    arrive(pool_r)
    got = whole.at[k, :, :, (b + 2) % NB]
    pool_c.append(start(got, got, partner))

    for copy, j in zip(refs_a, FAR_RING4):
        arrive([copy])
        got = refs.at[pl.ds(k * (REFS // 2) + ((a + NA - j) % NA) * 8, 8)]
        refs_c.append(start(got, got, partner))

    arrive(halos)
    arrive(pool_c)
    arrive(refs_c)
    for copy in sent:
        copy.wait_send()


def exchange(white, export, picked):
    vmem = pl.BlockSpec(memory_space=pltpu.VMEM)
    copies = 1 + 3 + 7 + 3 + 2 + 7 + 3 + 1 + 3 + 2 + 3 + 3 + 1 + 2 + 2 + 3 + 1
    return pl.pallas_call(
        exchange_kernel,
        name="exchange",
        in_specs=[vmem] * 3,
        out_specs=[vmem] * 3,
        out_shape=[
            jax.ShapeDtypeStruct((CH + 2 * HALO, ROWS, 128), BF),
            jax.ShapeDtypeStruct((2 * CH + 1, ROWS, 128), BF),
            jax.ShapeDtypeStruct((REFS, ROWS, 128), BF),
        ],
        scratch_shapes=[
            pltpu.VMEM((REFS // 2, ROWS, 128), BF),
            pltpu.VMEM((REFS // 2, ROWS, 128), BF),
            pltpu.VMEM((NA - 1, 8, ROWS, 128), BF),
            pltpu.VMEM((8, ROWS, 128), BF),
            pltpu.VMEM((NB - 1, 2, ROWS, 128), BF),
            pltpu.VMEM((2, ROWS, 128), BF),
            pltpu.VMEM((NZ - 1, 2, ROWS, 128), BF),
            pltpu.SemaphoreType.DMA((copies,)),
            pltpu.SemaphoreType.DMA((copies,)),
        ],
        compiler_params=pltpu.CompilerParams(
            collective_id=0, has_side_effects=True, vmem_limit_bytes=24 << 20
        ),
    )(white, export, picked)


def products(left, right, c):
    low = [[None] * 4 for _ in range(REFS // 16)]
    high = [[None] * 4 for _ in range(REFS // 16)]
    for t in range(4):
        lhs = [
            jnp.broadcast_to(left[c, row : row + 1, :], (16, 128)).astype(BF)
            for row in range(t, ROWS, 4)
        ]
        for r in range(REFS // 16):
            rhs = [right[row, r * 16 : r * 16 + 16, :] for row in range(t, ROWS, 4)]
            p = [u * v for u, v in zip(lhs, rhs)]
            q = [lhs[2 * s + 1] * rhs[2 * s] - lhs[2 * s] * rhs[2 * s + 1] for s in range(SEGS)]
            low[r][t] = ((p[0] + p[1]) + (p[2] + p[3])) + ((p[4] + p[5]) + (p[6] + p[7]))
            high[r][t] = (q[0] + q[1]) + (q[2] + q[3])
    return jnp.concatenate([jnp.concatenate(low[r] + high[r], 1) for r in range(REFS // 16)], 0)


def correlate_kernel(
    near, cross, mask, ext, pool, refs, table, out,
    index_rows, share_row, index, shares, wide, right, left, rows, load, store,
):
    base = (lax.axis_index("fibre") * (NZ * NA * NB) + lax.axis_index("chan")) * CH
    index_rows[0:NN, :] = near[...] - (base - HALO)
    p = cross[...]
    swapped = (p & ~15) | ((p & 3) << 2) | ((p >> 2) & 3)
    index_rows[NN : NN + XN, :] = jnp.where(mask[...] == 1, jnp.where(p < CH, p, swapped), 2 * CH)
    index_rows[NN + XN :, :] = jnp.zeros((16 - NN - XN, CH), jnp.int32)
    count = (1.0 + NN) + jnp.sum(mask[...].astype(F32), 0, keepdims=True)
    share_row[...] = 1.0 / count
    loads = [
        pltpu.make_async_copy(index_rows, index, load.at[0]),
        pltpu.make_async_copy(share_row, shares, load.at[1]),
    ]
    for copy in loads:
        copy.start()
    wide[...] = refs[...].astype(F32).reshape(REFS * ROWS, 128)
    for row in range(ROWS):
        right[row] = wide[pl.ds(row, REFS, stride=ROWS), :].astype(BF)
    for copy in loads:
        copy.wait()
    steps = CH // GROUP

    def put(step):
        return pltpu.make_async_copy(
            rows.at[step % 2], out.at[pl.ds(step * GROUP, GROUP)], store.at[step % 2]
        )

    def body(step, carry):
        for c in range(GROUP):
            chan = step * GROUP + c
            total = ext[HALO + chan].astype(F32)
            for n in range(NN):
                total = total + ext[index[n, chan]].astype(F32)
            for n in range(NN, NN + XN):
                total = total + pool[index[n, chan]].astype(F32)
            left[c] = (total * shares[0, chan]).astype(BF).astype(F32)

        @pl.when(step >= 2)
        def _():
            put(step - 2).wait()

        cross_spectra = [
            jnp.concatenate([products(left, right, c) for c in range(h, h + HALF)], 0)
            for h in range(0, GROUP, HALF)
        ]
        for h, spectrum in enumerate(cross_spectra):
            y = jnp.dot(spectrum, table[...], preferred_element_type=F32)
            rows[step % 2, h * HALF : (h + 1) * HALF] = y.astype(BF).reshape(HALF, REFS, LAGS)
        put(step).start()
        return carry

    lax.fori_loop(0, steps, body, 0)
    put(steps - 2).wait()
    put(steps - 1).wait()


def correlate(near_ids, cross_ids, cross_mask, ext, pool, refs):
    vmem = pl.BlockSpec(memory_space=pltpu.VMEM)
    hbm = pl.BlockSpec(memory_space=pl.ANY)
    return pl.pallas_call(
        correlate_kernel,
        name="correlate",
        in_specs=[vmem] * 7,
        out_specs=hbm,
        out_shape=jax.ShapeDtypeStruct((CH, REFS, LAGS), BF),
        scratch_shapes=[
            pltpu.VMEM((16, CH), jnp.int32),
            pltpu.VMEM((1, CH), F32),
            pltpu.SMEM((16, CH), jnp.int32),
            pltpu.SMEM((1, CH), F32),
            pltpu.VMEM((REFS * ROWS, 128), F32),
            pltpu.VMEM((ROWS, REFS, 128), BF),
            pltpu.VMEM((GROUP, ROWS, 128), F32),
            pltpu.VMEM((2, GROUP, REFS, LAGS), BF),
            pltpu.SemaphoreType.DMA((2,)),
            pltpu.SemaphoreType.DMA((2,)),
        ],
        compiler_params=pltpu.CompilerParams(vmem_limit_bytes=24 << 20),
    )(near_ids.T, cross_ids.T, cross_mask.T, ext, pool, refs, jnp.asarray(lag_table()))


def per_device(raw, starts, ref_ids, near_ids, cross_ids, cross_mask, export_loc):
    white, export, picked = spectra(ref_ids, starts, export_loc, raw)
    ext, pool, refs = exchange(white, export, picked)
    return correlate(near_ids, cross_ids, cross_mask, ext, pool, refs)


def solution(mesh):
    split = ("fibre", "chan")
    in_specs = (P(split, None), P(), P(), P(split, None), P(split, None), P(split, None), P(split))
    return jax.shard_map(
        per_device, mesh=mesh, in_specs=in_specs, out_specs=P(split, None, None), check_vma=False
    )
```

```python
import functools

import jax
import jax.numpy as jnp
import numpy as np
from jax import lax
from jax.experimental import pallas as pl
from jax.experimental.pallas import tpu as pltpu
from jax.sharding import PartitionSpec as P

SEG = 1024
SEGS = 4
REFS = 64
LAGS = 512
NN = 8
XN = 2
HALO = 16
CH = 128
NZ, NA, NB = 8, 4, 4
ROWS = SEGS * SEG // 128
GROUP = 16
HALF = 8
FAR_RING4 = (2, 1, 3)
FAR_RING8 = (4, 3, 5, 2, 6, 1, 7)
MESH = pl.DeviceIdType.MESH
BF = jnp.bfloat16
F32 = jnp.float32


def forward_table():
    phase = (np.arange(SEG)[:, None] * np.arange(SEG // 2)[None, :]) % SEG
    theta = phase * (2.0 * np.pi / SEG)
    keep = (np.arange(SEG // 2) > 0)[None, :]
    return np.concatenate([np.cos(theta) * keep, -np.sin(theta)], 1).astype(BF)


def lag_table():
    phase = (np.arange(SEG // 2)[:, None] * (np.arange(LAGS) - LAGS // 2)[None, :]) % SEG
    theta = phase * (2.0 * np.pi / SEG)
    scale = 1.0 / np.sqrt(SEG // 2)
    table = np.concatenate([np.cos(theta) * scale, -np.sin(theta) * scale], 0).astype(BF)
    return (table.astype(np.float32) / SEGS).astype(BF)


def spectra_kernel(ints_in, raw, table_in, white, export, picked, ints, samples, table, seg, wide, load):
    base = (lax.axis_index("fibre") * (NZ * NA * NB) + lax.axis_index("chan")) * CH
    loads = [
        pltpu.make_async_copy(raw, samples.at[:, pl.ds(0, SEGS * SEG)], load.at[0]),
        pltpu.make_async_copy(ints_in, ints, load.at[1]),
        pltpu.make_async_copy(table_in, table, load.at[2]),
    ]
    for copy in loads:
        copy.start()
    samples[:, SEGS * SEG :] = jnp.zeros((CH, 128), BF)
    loads[0].wait()
    loads[1].wait()
    for s in range(SEGS):
        begin = ints[REFS + s]
        lead = pl.multiple_of((begin // 128) * 128, 128)
        offset = begin - lead
        turned = [
            pltpu.roll(
                samples[:, pl.ds(lead + j * 128, 128)].astype(F32), (128 - offset) % 128, 1
            )
            for j in range(SEG // 128 + 1)
        ]
        here = lax.broadcasted_iota(jnp.int32, (CH, 128), 1) < 128 - offset
        for j in range(SEG // 128):
            cut = jnp.where(here, turned[j], turned[j + 1]).astype(BF)
            seg[s * CH : (s + 1) * CH, j * 128 : (j + 1) * 128] = cut
    loads[2].wait()
    for s in range(SEGS):
        spectrum = jnp.dot(
            seg[s * CH : (s + 1) * CH, :], table[...], preferred_element_type=F32
        )
        power = jnp.sum(spectrum * spectrum, -1, keepdims=True) / (SEG // 2)
        spectrum = spectrum / jnp.sqrt(power + 1e-06)
        for j in range(SEG // 128):
            wide[pl.ds(s * 8 + j, CH, stride=ROWS), :] = spectrum[:, j * 128 : (j + 1) * 128]

    def rows(channel):
        first = pl.multiple_of(channel * ROWS, ROWS)
        return wide[pl.ds(first, ROWS), :]

    def pick(r, carry):
        local = ints[r] - base
        mine = ((local >= 0) & (local < CH)).astype(F32)
        picked[r] = (rows(jnp.clip(local, 0, CH - 1)) * mine).astype(BF)
        return carry

    lax.fori_loop(0, REFS, pick, 0, unroll=8)
    export[0] = rows(ints[REFS + SEGS]).astype(BF)
    white[...] = wide[...].reshape(CH, ROWS, 128).astype(BF)


def spectra(ref_ids, starts, export_loc, raw):
    vmem = pl.BlockSpec(memory_space=pltpu.VMEM)
    hbm = pl.BlockSpec(memory_space=pl.ANY)
    fill = jnp.zeros((128 - REFS - SEGS - 1,), jnp.int32)
    ints = jnp.concatenate([ref_ids, starts, export_loc, fill])
    return pl.pallas_call(
        spectra_kernel,
        name="spectra",
        in_specs=[hbm] * 3,
        out_specs=[vmem] * 3,
        out_shape=[
            jax.ShapeDtypeStruct((CH, ROWS, 128), BF),
            jax.ShapeDtypeStruct((1, ROWS, 128), BF),
            jax.ShapeDtypeStruct((REFS, ROWS, 128), BF),
        ],
        scratch_shapes=[
            pltpu.SMEM((128,), jnp.int32),
            pltpu.VMEM((CH, SEGS * SEG + 128), BF),
            pltpu.VMEM((SEG, SEG), BF),
            pltpu.VMEM((CH * SEGS, SEG), BF),
            pltpu.VMEM((CH * ROWS, 128), F32),
            pltpu.SemaphoreType.DMA((3,)),
        ],
        compiler_params=pltpu.CompilerParams(vmem_limit_bytes=16 << 20),
    )(
        ints,
        pltpu.with_memory_space_constraint(raw, pltpu.HBM),
        pltpu.with_memory_space_constraint(jnp.asarray(forward_table()), pltpu.HBM),
    )


def exchange_kernel(
    white, export, picked, ext, pool, refs,
    core_in, half, a_in, a_sum, b_in, b_sum, z_in, send, recv,
):
    k = lax.axis_index("fibre")
    chan = lax.axis_index("chan")
    z, x, y = chan // (NA * NB), (chan // NB) % NA, chan % NB
    a = x * (1 - k) + y * k
    b = y * (1 - k) + x * k

    def at(zz, aa, bb):
        return zz * (NA * NB) + (aa * NB + bb) * (1 - k) + (bb * NB + aa) * k

    z_peer = [at((z + j) % NZ, a, b) for j in range(1, NZ)]
    a_peer = [at(z, (a + j) % NA, b) for j in range(1, NA)]
    b_peer = [at(z, a, (b + j) % NB) for j in range(1, NB)]
    up = (chan + 1) % (NZ * NA * NB)
    down = (chan + (NZ * NA * NB) - 1) % (NZ * NA * NB)
    own = z * (NA * NB) + a * NB + b

    barrier = pltpu.get_barrier_semaphore()
    peers = [(k, c) for c in z_peer + a_peer + b_peer + [up, down]] + [(1 - k, chan)]
    for peer in peers:
        pl.semaphore_signal(barrier, inc=1, device_id=peer, device_id_type=MESH)

    slot = [0]

    def start(src, dst, peer):
        i = slot[0]
        slot[0] += 1
        copy = pltpu.make_async_remote_copy(
            src_ref=src, dst_ref=dst, send_sem=send.at[i], recv_sem=recv.at[i],
            device_id=peer, device_id_type=MESH,
        )
        copy.start()
        return copy

    sent = []

    def arrive(copies):
        for copy in copies:
            copy.wait_recv()
        sent.extend(copies)

    partner = (1 - k, chan)
    whole = pool.at[pl.ds(0, 2 * CH)].reshape(2, NZ, NA, NB, ROWS, 128)

    pool[pl.ds(k * CH + own, 1)] = export[...]
    pool[pl.ds(2 * CH, 1)] = jnp.zeros((1, ROWS, 128), BF)
    pl.semaphore_wait(barrier, len(peers))
    core = start(picked.at[pl.ds((1 - k) * (REFS // 2), REFS // 2)], core_in, partner)
    mine = pool.at[pl.ds(k * CH + own, 1)]
    pool_z = [start(export, mine, (k, z_peer[j - 1])) for j in FAR_RING8]
    halos = [
        start(white.at[pl.ds(CH - HALO, HALO)], ext.at[pl.ds(0, HALO)], (k, up)),
        start(white.at[pl.ds(0, HALO)], ext.at[pl.ds(HALO + CH, HALO)], (k, down)),
    ]

    arrive([core])
    half[...] = picked[pl.ds(k * (REFS // 2), REFS // 2)] + core_in[...]
    a_rs = [
        start(half.at[pl.ds(((a + j) % NA) * 8, 8)], a_in.at[j - 1], (k, a_peer[j - 1]))
        for j in FAR_RING4
    ]

    arrive(pool_z)
    column = whole.at[k, :, a, b]
    pool_a = [start(column, column, (k, a_peer[j - 1])) for j in FAR_RING4]
    pool_c = [start(column, column, partner)]
    ext[HALO : HALO + CH] = white[...]

    arrive(a_rs)
    a_sum[...] = half[pl.ds(a * 8, 8)] + a_in[0] + a_in[1] + a_in[2]
    b_rs = [
        start(a_sum.at[pl.ds(((b + j) % NB) * 2, 2)], b_in.at[j - 1], (k, b_peer[j - 1]))
        for j in FAR_RING4
    ]

    arrive(b_rs)
    b_sum[...] = a_sum[pl.ds(b * 2, 2)] + b_in[0] + b_in[1] + b_in[2]
    z_rs = [start(b_sum, z_in.at[j - 1], (k, z_peer[j - 1])) for j in FAR_RING8]

    arrive(pool_a)
    plane = whole.at[k, :, :, b]
    pool_b = [start(plane, plane, (k, b_peer[0])), start(plane, plane, (k, b_peer[2]))]
    for j in range(1, NA):
        got = whole.at[k, :, (a + NA - j) % NA, b]
        pool_c.append(start(got, got, partner))

    arrive(z_rs)
    total = b_sum[...]
    for j in range(NZ - 1):
        total = total + z_in[j]
    lead = k * (REFS // 2) + a * 8
    pair = refs.at[pl.ds(lead + b * 2, 2)]
    refs[pl.ds(lead + b * 2, 2)] = total
    refs_b = [start(pair, pair, (k, b_peer[j - 1])) for j in FAR_RING4]

    arrive(pool_b)
    low = whole.at[k, pl.ds(0, NZ // 2), :, (b + NB - 1) % NB]
    high = whole.at[k, pl.ds(NZ // 2, NZ // 2), :, (b + 1) % NB]
    pool_r = [start(low, low, (k, b_peer[0])), start(high, high, (k, b_peer[2]))]

    arrive(refs_b)
    eight = refs.at[pl.ds(lead, 8)]
    refs_a = [start(eight, eight, (k, a_peer[j - 1])) for j in FAR_RING4]
    refs_c = [start(eight, eight, partner)]
    for c in ((b + NB - 1) % NB, (b + 1) % NB):
        got = whole.at[k, :, :, c]
        pool_c.append(start(got, got, partner))

    arrive(pool_r)
    got = whole.at[k, :, :, (b + 2) % NB]
    pool_c.append(start(got, got, partner))

    for copy, j in zip(refs_a, FAR_RING4):
        arrive([copy])
        got = refs.at[pl.ds(k * (REFS // 2) + ((a + NA - j) % NA) * 8, 8)]
        refs_c.append(start(got, got, partner))

    arrive(halos)
    arrive(pool_c)
    arrive(refs_c)
    for copy in sent:
        copy.wait_send()


def exchange(white, export, picked):
    vmem = pl.BlockSpec(memory_space=pltpu.VMEM)
    copies = 1 + 3 + 7 + 3 + 2 + 7 + 3 + 1 + 3 + 2 + 3 + 3 + 1 + 2 + 2 + 3 + 1
    return pl.pallas_call(
        exchange_kernel,
        name="exchange",
        in_specs=[vmem] * 3,
        out_specs=[vmem] * 3,
        out_shape=[
            jax.ShapeDtypeStruct((CH + 2 * HALO, ROWS, 128), BF),
            jax.ShapeDtypeStruct((2 * CH + 1, ROWS, 128), BF),
            jax.ShapeDtypeStruct((REFS, ROWS, 128), BF),
        ],
        scratch_shapes=[
            pltpu.VMEM((REFS // 2, ROWS, 128), BF),
            pltpu.VMEM((REFS // 2, ROWS, 128), BF),
            pltpu.VMEM((NA - 1, 8, ROWS, 128), BF),
            pltpu.VMEM((8, ROWS, 128), BF),
            pltpu.VMEM((NB - 1, 2, ROWS, 128), BF),
            pltpu.VMEM((2, ROWS, 128), BF),
            pltpu.VMEM((NZ - 1, 2, ROWS, 128), BF),
            pltpu.SemaphoreType.DMA((copies,)),
            pltpu.SemaphoreType.DMA((copies,)),
        ],
        compiler_params=pltpu.CompilerParams(
            collective_id=0, has_side_effects=True, vmem_limit_bytes=24 << 20
        ),
    )(white, export, picked)


def products(left, right, c):
    low = [[None] * 4 for _ in range(REFS // 16)]
    high = [[None] * 4 for _ in range(REFS // 16)]
    for t in range(4):
        lhs = [
            jnp.broadcast_to(left[c, row : row + 1, :], (16, 128)).astype(BF)
            for row in range(t, ROWS, 4)
        ]
        for r in range(REFS // 16):
            rhs = [right[row, r * 16 : r * 16 + 16, :] for row in range(t, ROWS, 4)]
            p = [u * v for u, v in zip(lhs, rhs)]
            q = [lhs[2 * s + 1] * rhs[2 * s] - lhs[2 * s] * rhs[2 * s + 1] for s in range(SEGS)]
            low[r][t] = ((p[0] + p[1]) + (p[2] + p[3])) + ((p[4] + p[5]) + (p[6] + p[7]))
            high[r][t] = (q[0] + q[1]) + (q[2] + q[3])
    return jnp.concatenate([jnp.concatenate(low[r] + high[r], 1) for r in range(REFS // 16)], 0)


def correlate_kernel(
    near, cross, mask, ext, pool, refs, table, out,
    index_rows, share_row, index, shares, wide, right, left, rows, load, store,
):
    base = (lax.axis_index("fibre") * (NZ * NA * NB) + lax.axis_index("chan")) * CH
    index_rows[0:NN, :] = near[...] - (base - HALO)
    p = cross[...]
    swapped = (p & ~15) | ((p & 3) << 2) | ((p >> 2) & 3)
    index_rows[NN : NN + XN, :] = jnp.where(mask[...] == 1, jnp.where(p < CH, p, swapped), 2 * CH)
    index_rows[NN + XN :, :] = jnp.zeros((16 - NN - XN, CH), jnp.int32)
    count = (1.0 + NN) + jnp.sum(mask[...].astype(F32), 0, keepdims=True)
    share_row[...] = 1.0 / count
    loads = [
        pltpu.make_async_copy(index_rows, index, load.at[0]),
        pltpu.make_async_copy(share_row, shares, load.at[1]),
    ]
    for copy in loads:
        copy.start()
    wide[...] = refs[...].astype(F32).reshape(REFS * ROWS, 128)
    for row in range(ROWS):
        right[row] = wide[pl.ds(row, REFS, stride=ROWS), :].astype(BF)
    for copy in loads:
        copy.wait()
    steps = CH // GROUP

    def put(step):
        return pltpu.make_async_copy(
            rows.at[step % 2], out.at[pl.ds(step * GROUP, GROUP)], store.at[step % 2]
        )

    def smooth(step):
        for c in range(GROUP):
            chan = step * GROUP + c
            total = ext[HALO + chan].astype(F32)
            for n in range(NN):
                total = total + ext[index[n, chan]].astype(F32)
            for n in range(NN, NN + XN):
                total = total + pool[index[n, chan]].astype(F32)
            left[c] = (total * shares[0, chan]).astype(BF).astype(F32)

    def body(step, carry):
        @pl.when(step >= 2)
        def _():
            put(step - 2).wait()

        cross_spectra = [
            jnp.concatenate([products(left, right, c) for c in range(h, h + HALF)], 0)
            for h in range(0, GROUP, HALF)
        ]
        smooth(jnp.minimum(step + 1, steps - 1))
        for h, spectrum in enumerate(cross_spectra):
            y = jnp.dot(spectrum, table[...], preferred_element_type=F32)
            rows[step % 2, h * HALF : (h + 1) * HALF] = y.astype(BF).reshape(HALF, REFS, LAGS)
        put(step).start()
        return carry

    smooth(0)
    lax.fori_loop(0, steps, body, 0)
    put(steps - 2).wait()
    put(steps - 1).wait()


def correlate(near_ids, cross_ids, cross_mask, ext, pool, refs):
    vmem = pl.BlockSpec(memory_space=pltpu.VMEM)
    hbm = pl.BlockSpec(memory_space=pl.ANY)
    return pl.pallas_call(
        correlate_kernel,
        name="correlate",
        in_specs=[vmem] * 7,
        out_specs=hbm,
        out_shape=jax.ShapeDtypeStruct((CH, REFS, LAGS), BF),
        scratch_shapes=[
            pltpu.VMEM((16, CH), jnp.int32),
            pltpu.VMEM((1, CH), F32),
            pltpu.SMEM((16, CH), jnp.int32),
            pltpu.SMEM((1, CH), F32),
            pltpu.VMEM((REFS * ROWS, 128), F32),
            pltpu.VMEM((ROWS, REFS, 128), BF),
            pltpu.VMEM((GROUP, ROWS, 128), F32),
            pltpu.VMEM((2, GROUP, REFS, LAGS), BF),
            pltpu.SemaphoreType.DMA((2,)),
            pltpu.SemaphoreType.DMA((2,)),
        ],
        compiler_params=pltpu.CompilerParams(vmem_limit_bytes=24 << 20),
    )(near_ids.T, cross_ids.T, cross_mask.T, ext, pool, refs, jnp.asarray(lag_table()))


def per_device(raw, starts, ref_ids, near_ids, cross_ids, cross_mask, export_loc):
    white, export, picked = spectra(ref_ids, starts, export_loc, raw)
    ext, pool, refs = exchange(white, export, picked)
    return correlate(near_ids, cross_ids, cross_mask, ext, pool, refs)


def solution(mesh):
    split = ("fibre", "chan")
    in_specs = (P(split, None), P(), P(), P(split, None), P(split, None), P(split, None), P(split))
    return jax.shard_map(
        per_device, mesh=mesh, in_specs=in_specs, out_specs=P(split, None, None), check_vma=False
    )
```
